256 devices in a mesh: group: 2 (over core), fsdp: 32 (over x, z), tp: 4 (over y).
Axes of the slice: x: 4, y: 4, z: 8, core: 2. Of those that a mesh axis runs over, the one named last changes fastest.
Arguments:
- text_embeds: bfloat16 [32768, 8192], P(('group', 'fsdp'), 'tp'), may hold values from -16 to 16
- image_embeds: bfloat16 [16384, 8192], P(('group', 'fsdp'), 'tp'), may hold values from -6 to 6
- key_weight: bfloat16 [8192, 512], P(('group', 'fsdp')), may hold values from -0.0625 to 0.0625
- key_bias: float32 [512], P('tp'), may hold values from -3 to 3
- key_cot: bfloat16 [32768, 512], P(('group', 'fsdp')), may hold values from -6 to 6
- image_owner: int32 [16384], P(('group', 'fsdp')), may hold values from 0 to 63, as said below
- image_slot: int32 [32768], P(('group', 'fsdp')), may hold values from -1 to 511, as said below
- seq_lengths: int32 [128], P(('group', 'fsdp')), may hold values from 248 to 256, as said below
Outputs:
- key_rows: bfloat16 [32768, 512], P(('group', 'fsdp'), 'tp')
- text_grad: bfloat16 [32768, 8192], P(('group', 'fsdp'), 'tp')
- image_grad: bfloat16 [16384, 8192], P(('group', 'fsdp'), 'tp')
- weight_grad: float32 [8192, 512], P(('group', 'fsdp'), 'tp')
The draws below stay inside these ranges and needn't reach their ends.
Inputs may be any that keep to these rules, and one draw needn't show every extreme that they name: `image_owner`: A source block of 256 image tokens sends at most 8 of them to one owner, and some block sends exactly 8 to some owner; an owner takes at most 448 image tokens in all, and some owner takes exactly that many. Every image token has exactly one position, as step one says. `image_slot`: slots are distinct within an owner block, and image tokens sit only at live positions. `seq_lengths`: some sequence has length 256.
All inputs are finite; a program needn't handle non-finite values.
Results may differ from the reference program's by a relative error of at most 0.0046.
Values may be sent and summed in bfloat16 or wider, within the bound.
No kernel may reach another device: no remote copies, remote signals or barrier semaphores. Data moves between devices by JAX's collectives and lax.ppermute only.
A program may use at most 64 MiB of HBM per device.

```python
import jax
import jax.numpy as jnp
from jax import lax

D = 8192
HEAD_DIM = 128
LENGTH = 256
SEQ_DEV = 2
KW = 512
UNITS = 64
LANG_DEV = 512
IMG_DEV = 256
CAP = 8
LANG_TOKENS = 32768
IMG_TOKENS = 16384


def layout_tables(key):
    base_key = jax.random.fold_in(key, 9137)
    subkeys = jax.random.split(base_key, 8)
    unit_count = UNITS
    quantum = LANG_DEV // (8 * UNITS)
    ordinal = jnp.arange(unit_count, dtype=jnp.int32)
    heavy_count = jax.random.randint(subkeys[0], (), 1, unit_count // 2 + 1)
    light_count = jax.random.randint(subkeys[1], (), 1, unit_count // 2 + 1)
    owner_sorted = jnp.where(ordinal < heavy_count, 6 * quantum, jnp.where(ordinal < unit_count - heavy_count, 3 * quantum, 0)).astype(jnp.int32)
    offset_sorted = jnp.where(ordinal < light_count, 2 * quantum, jnp.where(ordinal < unit_count - light_count, quantum, 0)).astype(jnp.int32)
    owner_load = owner_sorted[jax.random.permutation(subkeys[2], unit_count)]
    offset_load = offset_sorted[jax.random.permutation(subkeys[3], unit_count)]
    shift_index = (ordinal[None, :] - ordinal[:, None]) % unit_count
    counts = (owner_load[None, :] + offset_load[shift_index]).astype(jnp.int32)
    cum_owner = jnp.cumsum(counts, axis=1)
    token_index = jnp.arange(IMG_DEV, dtype=jnp.int32)
    owner_list = jnp.sum((cum_owner[:, None, :] <= token_index[None, :, None]).astype(jnp.int32), axis=2)
    row_keys = jax.random.split(subkeys[4], unit_count)
    row_perms = jax.vmap(lambda one_key: jax.random.permutation(one_key, IMG_DEV))(row_keys)
    owners = jnp.take_along_axis(owner_list, row_perms, axis=1).astype(jnp.int32)
    seq_total = unit_count * SEQ_DEV
    padding = jax.random.randint(subkeys[5], (seq_total,), 0, LENGTH // 32 + 1)
    full_one = jax.random.randint(subkeys[6], (), 0, seq_total)
    lengths = (LENGTH - jnp.where(jnp.arange(seq_total) == full_one, 0, padding)).astype(jnp.int32)
    within = jnp.arange(LANG_DEV, dtype=jnp.int32)
    live_table = within[None, :] % LENGTH < lengths.reshape(unit_count, SEQ_DEV)[:, within // LENGTH]
    place_keys = jax.random.split(subkeys[7], unit_count)
    place_perms = jax.vmap(lambda one_key: jax.random.permutation(one_key, LANG_DEV))(place_keys)
    live_perm = jnp.take_along_axis(live_table, place_perms, axis=1)
    arrival = jnp.cumsum(live_perm.astype(jnp.int32), axis=1) - 1
    incoming = jnp.sum(counts, axis=0)
    chosen = live_perm & (arrival < incoming[:, None])
    cum_source = jnp.cumsum(counts, axis=0).T
    source_ids = jnp.sum((cum_source[:, None, :] <= arrival[:, :, None]).astype(jnp.int32), axis=2)
    source_ids = jnp.clip(source_ids, 0, unit_count - 1)
    start_table = (jnp.cumsum(counts, axis=0) - counts).T
    source_start = jnp.take_along_axis(start_table, source_ids, axis=1)
    slot_value = jnp.where(chosen, source_ids * CAP + arrival - source_start, -1).astype(jnp.int32)
    slots = jnp.zeros((unit_count, LANG_DEV), jnp.int32).at[ordinal[:, None], place_perms].set(slot_value)
    return (owners.reshape(-1), slots.reshape(-1), lengths)


def draw_image_owner(key, part):
    return layout_tables(key)[0]


def draw_image_slot(key, part):
    return layout_tables(key)[1]


def draw_seq_lengths(key, part):
    return layout_tables(key)[2]


def spiked(values, rng, source, target, shards_of, factor):
    def block_of(dim):
        return (jnp.arange(values.shape[dim]) // (values.shape[dim] // shards_of)).reshape((-1,) + (1,) * (values.ndim - 1 - dim))

    near = jax.random.permutation(rng, shards_of)[block_of(target)]
    second = (block_of(target) + shards_of // 2) % shards_of
    return jnp.where((block_of(source) == near) | (block_of(source) == second), factor * values, values)


def levels(rng, dims, cuts, least, high):
    def one(axis_at, blocks):
        steps = jax.random.uniform(jax.random.fold_in(jax.random.fold_in(rng, 6), axis_at), (blocks,), jnp.float32, least / len(cuts), high / len(cuts))
        return jnp.repeat(jnp.exp(steps), dims[axis_at] // blocks).reshape((-1,) + (1,) * (len(dims) - axis_at - 1))

    factor_of = one(*cuts[0])
    for cut in cuts[1:]:
        factor_of = factor_of * one(*cut)
    return factor_of


def bell_draw(stream_key, shape, width, limit, cuts=(), kind=jnp.bfloat16):
    loudness = levels(stream_key, shape, cuts, -0.22, 0.18) if cuts else 1.0
    drawn = jax.random.normal(stream_key, shape, jnp.float32) * width * loudness
    return jnp.minimum(jnp.maximum(drawn, -limit), limit).astype(kind)


def heavy_noise(own_key, extent, width, reach, shards, heavy, held_as=jnp.bfloat16):
    result = width * jax.random.normal(own_key, extent, jnp.float32)
    if shards:
        result = result * levels(own_key, extent, shards, -0.22, 0.18)
    return jnp.clip(spiked(result, jax.random.fold_in(own_key, 3), *heavy), -reach, reach).astype(held_as)


def setup_inputs(seed: int = 0) -> dict:
    key_list = jax.random.split(jax.random.key(seed), 9)
    return {
        "text_embeds": heavy_noise(key_list[0], (LANG_TOKENS, D), 1.0, 16.0, ((0, 64), (1, 4)), (0, 1, 64, 4.0)),
        "image_embeds": bell_draw(key_list[1], (IMG_TOKENS, D), 1.0, 6.0, ((0, 64), (1, 4))),
        "key_weight": bell_draw(key_list[2], (D, KW), D ** -0.5, 0.0625, ((0, 64),)),
        "key_bias": bell_draw(key_list[3], (KW,), 0.5, 3.0, ((0, 4),), jnp.float32),
        "key_cot": bell_draw(key_list[4], (LANG_TOKENS, KW), 1.0, 6.0, ((0, 64),)),
        "image_owner": draw_image_owner(jax.random.fold_in(key_list[8], 71), 0),
        "image_slot": draw_image_slot(jax.random.fold_in(key_list[8], 71), 0),
        "seq_lengths": draw_seq_lengths(jax.random.fold_in(key_list[8], 71), 0),
    }


ROPE_BASE = 1000000.0


def angles(row_total):
    position = (jnp.arange(row_total, dtype=jnp.int32) % LENGTH).astype(jnp.float32)
    frequency = ROPE_BASE ** (-(jnp.arange(HEAD_DIM // 2, dtype=jnp.float32) * 2.0) / HEAD_DIM)
    angle_table = position[:, None] * frequency[None, :]
    return jnp.cos(angle_table), jnp.sin(angle_table)


def rotate(values, cosine, sine, direction):
    row_total = values.shape[0]
    by_head = values.reshape(row_total, -1, HEAD_DIM)
    half_dim = HEAD_DIM // 2
    front_half = by_head[..., :half_dim]
    second = by_head[..., half_dim:]
    cos_part = cosine[:, None, :]
    sin_part = direction * sine[:, None, :]
    rotated = jnp.concatenate([front_half * cos_part - second * sin_part, second * cos_part + front_half * sin_part], axis=-1)
    return rotated.reshape(row_total, -1)


def reference(text_embeds, image_embeds, key_weight, key_bias, key_cot, image_owner, image_slot, seq_lengths):
    unit_count = UNITS
    owners = image_owner.reshape(unit_count, IMG_DEV)
    ordinal = jnp.arange(unit_count, dtype=jnp.int32)
    marks = (owners[:, :, None] == ordinal[None, None, :]).astype(jnp.int32)
    before = jnp.cumsum(marks, axis=1) - marks
    owner_rank = jnp.sum(before * marks, axis=2)
    destination = owners * (unit_count * CAP) + ordinal[:, None] * CAP + owner_rank
    source_table = jnp.zeros((unit_count * unit_count * CAP,), jnp.int32).at[destination.reshape(-1)].set(jnp.arange(unit_count * IMG_DEV, dtype=jnp.int32))
    slots = image_slot.reshape(unit_count, LANG_DEV)
    is_image = (slots >= 0).reshape(-1)
    lookup = (ordinal[:, None] * (unit_count * CAP) + jnp.maximum(slots, 0)).reshape(-1)
    image_row = source_table[lookup]
    hidden = jnp.where(is_image[:, None], image_embeds[image_row], text_embeds)
    position = jnp.arange(LANG_TOKENS, dtype=jnp.int32)
    live_mask = ((position % LENGTH) < seq_lengths[position // LENGTH]).astype(jnp.float32)
    cosine, sine = angles(LANG_TOKENS)
    projected = jnp.dot(hidden, key_weight, preferred_element_type=jnp.float32) + key_bias
    key_rows = (rotate(projected, cosine, sine, 1.0) * live_mask[:, None]).astype(jnp.bfloat16)
    masked = key_cot.astype(jnp.float32) * live_mask[:, None]
    rotated_back = rotate(masked, cosine, sine, -1.0).astype(jnp.bfloat16)
    hidden_grad = lax.dot_general(rotated_back, key_weight, (((1,), (1,)), ((), ())), preferred_element_type=jnp.float32).astype(jnp.bfloat16)
    text_grad = jnp.where(is_image[:, None], jnp.zeros_like(hidden_grad), hidden_grad)
    token_place = jnp.zeros((unit_count * IMG_DEV,), jnp.int32).at[jnp.where(is_image, image_row, unit_count * IMG_DEV)].set(position, mode="drop")
    image_grad = hidden_grad[token_place]
    weight_grad = lax.dot_general(hidden, rotated_back, (((0,), (0,)), ((), ())), preferred_element_type=jnp.float32) / LANG_DEV
    return key_rows, text_grad, image_grad, weight_grad
```

```python
import jax
import jax.numpy as jnp
import numpy as np
from jax import lax
from jax.sharding import Mesh
from jax.sharding import PartitionSpec as P

HEAD_DIM = 128
LENGTH = 256
GROUP_FSDP = ("group", "fsdp_0", "fsdp_1")
ALL = ("group", "fsdp_0", "fsdp_1", "tp")
NX, NZ, NT = 4, 8, 4

ROPE_BASE = 1000000.0


def spread_pairs():
    pairs = []
    for g in range(2):
        for x in range(NX):
            for z in range(NZ):
                for t in range(NT):
                    plane = 2 * g + x // 2
                    to_x = 2 * (t // 2) + x % 2
                    source = ((g * NX + x) * NZ + z) * NT + t
                    target = (((t % 2) * NX + to_x) * NZ + z) * NT + plane
                    pairs.append((source, target))
    return pairs


SPREAD = spread_pairs()
GATHER = [(b, a) for a, b in SPREAD]
SWAP = [(0, 1), (1, 0)]


def to_all(array, axis):
    return lax.all_to_all(array, axis, split_axis=0, concat_axis=0, tiled=True)


def copies(array, axis):
    count = lax.axis_size(axis)
    return to_all(jnp.broadcast_to(array[None], (count, *array.shape)), axis)


def tables():
    position = np.arange(LENGTH, dtype=np.float64)
    frequency = ROPE_BASE ** (-(np.arange(HEAD_DIM // 2) * 2.0) / HEAD_DIM)
    angle = position[:, None] * frequency[None, :]
    cosine, sine = np.cos(angle), np.sin(angle)
    whole = np.concatenate([cosine, cosine], axis=1).astype(np.float32)
    signed = np.concatenate([-sine, sine], axis=1).astype(np.float32)
    return whole, signed


def rotate(values, direction):
    whole, signed = tables()
    rows = values.shape[0]
    by_head = values.reshape(rows // LENGTH, LENGTH, -1, HEAD_DIM)
    half = HEAD_DIM // 2
    swapped = jnp.concatenate([by_head[..., half:], by_head[..., :half]], axis=-1)
    turned = by_head * whole[None, :, None, :] + swapped * (direction * signed)[None, :, None, :]
    return turned.reshape(rows, -1)


def exact_rows(marks, values):
    return jnp.dot(
        marks.astype(jnp.bfloat16), values, preferred_element_type=jnp.float32
    ).astype(jnp.bfloat16)


def per_device(
    text_embeds, image_embeds, key_weight, key_bias, key_cot, image_owner, image_slot, seq_lengths
):
    rows, columns = text_embeds.shape
    tokens = image_embeds.shape[0]
    units = lax.axis_size(GROUP_FSDP)
    slots = rows
    capacity = slots // units
    g = lax.axis_index("group")
    t = lax.axis_index("tp")
    bf = jnp.bfloat16

    own = lax.dynamic_slice_in_dim(key_weight, t * HEAD_DIM, HEAD_DIM, 1)
    piece = lax.ppermute(own, ALL, SPREAD)
    along_z = copies(piece, "fsdp_1").reshape(NZ * 128, HEAD_DIM)
    along_x = copies(along_z, "fsdp_0")
    other = lax.ppermute(along_x, "group", SWAP)
    even = jnp.where(g == 0, along_x, other)
    odd = jnp.where(g == 0, other, along_x)
    both = jnp.stack([even, odd]).reshape(2, 2, 2, NZ * 128, HEAD_DIM)
    weight = both.transpose(2, 3, 1, 0, 4).reshape(columns, 4 * HEAD_DIM)

    position = jnp.arange(rows, dtype=jnp.int32)
    limits = jnp.repeat(seq_lengths, LENGTH, total_repeat_length=rows)
    live = position % LENGTH < limits
    live_mask = live.astype(jnp.float32)
    is_image = image_slot >= 0
    back = rotate(key_cot.astype(jnp.float32) * live_mask[:, None], -1.0).astype(bf)
    slot_ids = jnp.arange(slots, dtype=jnp.int32)
    by_slot = exact_rows(slot_ids[:, None] == image_slot[None, :], back)
    arrived = to_all(by_slot.reshape(units, capacity, -1), GROUP_FSDP).reshape(slots, -1)
    order = jnp.arange(tokens, dtype=jnp.int32)
    same = (image_owner[:, None] == image_owner[None, :]) & (order[None, :] < order[:, None])
    slot_of = image_owner * capacity + jnp.sum(same.astype(jnp.int32), axis=1)
    back_image = exact_rows(slot_of[:, None] == slot_ids[None, :], arrived)
    back_text = jnp.where(is_image[:, None], jnp.zeros_like(back), back)

    def halves(array):
        parts = array.reshape(array.shape[0], 2, 2, HEAD_DIM)
        mine = jnp.where(g == 0, parts[:, :, 0], parts[:, :, 1])
        yours = jnp.where(g == 0, parts[:, :, 1], parts[:, :, 0])
        return mine.reshape(-1, 2 * HEAD_DIM), yours.reshape(-1, 2 * HEAD_DIM)

    def grad_terms(text_part, image_part):
        dims = (((0,), (0,)), ((), ()))
        return lax.dot_general(
            text_embeds, text_part, dims, preferred_element_type=jnp.float32
        ) + lax.dot_general(image_embeds, image_part, dims, preferred_element_type=jnp.float32)

    text_mine, text_yours = halves(back_text)
    image_mine, image_yours = halves(back_image)
    given = lax.ppermute(grad_terms(text_yours, image_yours).astype(bf), "group", SWAP)
    chip = grad_terms(text_mine, image_mine) + given.astype(jnp.float32)
    chip = chip.astype(bf).reshape(2, NZ * 128, 2, HEAD_DIM).transpose(2, 0, 1, 3)
    over_x = to_all(chip.reshape(4, NZ * 128, HEAD_DIM), "fsdp_0")
    over_x = over_x.astype(jnp.float32).sum(axis=0).astype(bf)
    over_z = to_all(over_x.reshape(NZ, 128, HEAD_DIM), "fsdp_1")
    over_z = over_z.astype(jnp.float32).sum(axis=0) / rows
    weight_grad = lax.ppermute(over_z, ALL, GATHER)

    def terms(values):
        parts = jnp.dot(values, weight, preferred_element_type=jnp.float32).astype(bf)
        return parts.reshape(-1, NT, HEAD_DIM).transpose(1, 0, 2)

    parts = jnp.concatenate([terms(text_embeds), terms(image_embeds)], axis=1)
    keys = to_all(parts, "tp").astype(jnp.float32).sum(axis=0)
    keys_text, keys_image = keys[:rows], keys[rows:].astype(bf)
    image_by_slot = exact_rows(slot_ids[:, None] == slot_of[None, :], keys_image)
    came = to_all(image_by_slot.reshape(units, capacity, HEAD_DIM), GROUP_FSDP)
    placed = jnp.dot(
        (image_slot[:, None] == slot_ids[None, :]).astype(bf),
        came.reshape(slots, HEAD_DIM),
        preferred_element_type=jnp.float32,
    )
    projected = jnp.where(is_image[:, None], placed, keys_text) + key_bias
    key_rows = (rotate(projected, 1.0) * live_mask[:, None]).astype(bf)

    def spread_back(values):
        return lax.dot_general(
            values, weight, (((1,), (1,)), ((), ())), preferred_element_type=jnp.float32
        ).astype(bf)

    return key_rows, spread_back(back_text), spread_back(back_image), weight_grad


def solution(mesh):
    split = Mesh(
        mesh.devices.reshape(mesh.shape["group"], NX, NZ, mesh.shape["tp"]),
        ("group", "fsdp_0", "fsdp_1", "tp"),
    )
    wide = P(GROUP_FSDP, "tp")
    return jax.shard_map(
        per_device,
        mesh=split,
        in_specs=(
            wide,
            wide,
            P(GROUP_FSDP, None),
            P("tp"),
            P(GROUP_FSDP, None),
            P(GROUP_FSDP),
            P(GROUP_FSDP),
            P(GROUP_FSDP),
        ),
        out_specs=(wide, wide, wide, wide),
        check_vma=False,
    )
```

```python
import jax
import jax.numpy as jnp
import numpy as np
from jax import lax
from jax.experimental import pallas as pl
from jax.experimental.pallas import tpu as pltpu
from jax.sharding import Mesh
from jax.sharding import PartitionSpec as P


HEAD_DIM = 128
LENGTH = 256
GROUP_FSDP = ("group", "fsdp_0", "fsdp_1")
ALL = ("group", "fsdp_0", "fsdp_1", "tp")
NX, NZ, NT = 4, 8, 4

ROPE_BASE = 1000000.0


def spread_pairs():
    pairs = []
    for g in range(2):
        for x in range(NX):
            for z in range(NZ):
                for t in range(NT):
                    plane = 2 * g + x // 2
                    to_x = 2 * (t // 2) + x % 2
                    source = ((g * NX + x) * NZ + z) * NT + t
                    target = (((t % 2) * NX + to_x) * NZ + z) * NT + plane
                    pairs.append((source, target))
    return pairs


SPREAD = spread_pairs()
GATHER = [(b, a) for a, b in SPREAD]
SWAP = [(0, 1), (1, 0)]


def to_all(array, axis):
    return lax.all_to_all(array, axis, split_axis=0, concat_axis=0, tiled=True)


def ring(axis, step):
    count = lax.axis_size(axis)
    return [(i, (i + step) % count) for i in range(count)]


def shifted(array, axis, step):
    return lax.ppermute(array, axis, ring(axis, step))


def tables():
    position = np.arange(LENGTH, dtype=np.float64)
    frequency = ROPE_BASE ** (-(np.arange(HEAD_DIM // 2) * 2.0) / HEAD_DIM)
    angle = position[:, None] * frequency[None, :]
    cosine, sine = np.cos(angle), np.sin(angle)
    whole = np.concatenate([cosine, cosine], axis=1).astype(np.float32)
    signed = np.concatenate([-sine, sine], axis=1).astype(np.float32)
    return jnp.asarray(whole), jnp.asarray(signed)


ALL_VMEM, SOME_VMEM = 67043328, 20 << 20
IN_HBM = ("back", "take", "grads", "finish", "keys")
BF, F32, I32 = jnp.bfloat16, jnp.float32, jnp.int32
VMEM = pl.BlockSpec(memory_space=pltpu.VMEM)
SMEM = pl.BlockSpec(memory_space=pltpu.SMEM)


def shape(*dims, dtype=BF):
    return jax.ShapeDtypeStruct(dims, dtype)


def cost(flops, size):
    return pl.CostEstimate(flops=flops, bytes_accessed=size, transcendentals=0)


def kernel_call(body, name, **settings):
    limits = pltpu.CompilerParams(vmem_limit_bytes=ALL_VMEM if name in IN_HBM else SOME_VMEM)
    return pl.pallas_call(body, compiler_params=limits, **settings)


def mm(a, b):
    return jnp.dot(a, b, preferred_element_type=F32)


def ones_where(condition):
    return jnp.where(condition, 1.0, 0.0).astype(BF)


def flip(array):
    return array.astype(F32).T.astype(BF)


def back_kernel(seq_ref, slot_ref, cot_ref, whole_ref, signed_ref, back_ref, sent_ref, full_ref):
    t = lax.axis_index("tp")
    rows = cot_ref.shape[0]
    slot_row = slot_ref[...]
    is_image = jnp.broadcast_to(slot_row, (HEAD_DIM, rows)).T >= 0
    for s in range(rows // LENGTH):
        part = slice(s * LENGTH, (s + 1) * LENGTH)
        live = lax.broadcasted_iota(I32, (LENGTH, HEAD_DIM), 0) < seq_ref[s]
        for h in range(4):
            value = cot_ref[part, h * HEAD_DIM : (h + 1) * HEAD_DIM].astype(F32)
            value = jnp.where(live, value, 0.0)
            turned = value * whole_ref[...] - pltpu.roll(value, HEAD_DIM // 2, 1) * signed_ref[...]
            full_ref[h, part] = turned.astype(BF)
            back_ref[h, part] = jnp.where(is_image[part], 0.0, turned).astype(BF)
    line = lax.broadcasted_iota(I32, (rows, rows), 0)
    sent_ref[...] = mm(ones_where(line == slot_row), full_ref[t]).astype(BF)


def ranks(owner_ref, axis):
    tokens = owner_ref.shape[1]
    across = jnp.broadcast_to(owner_ref[...], (tokens, tokens))
    down = across.T
    first = lax.broadcasted_iota(I32, (tokens, tokens), 0)
    second = lax.broadcasted_iota(I32, (tokens, tokens), 1)
    before = second < first if axis == 1 else first < second
    same = jnp.where((across == down) & before, 1.0, 0.0)
    owner = down[:, :1] if axis == 1 else across[:1]
    return owner, jnp.sum(same, axis=axis, keepdims=True).astype(I32)


def parted(block):
    away = ((block >> 5) + lax.axis_index("group")) & 1
    return (block >> 3) & 3, block & 7, away


def take_kernel(owner_ref, came_ref, out_ref):
    owner, rank = ranks(owner_ref, 1)
    lanes = lax.broadcasted_iota(I32, (owner.shape[0], came_ref.shape[0]), 1)
    out_ref[...] = mm(ones_where(lanes == owner * 8 + rank), came_ref[...]).astype(BF)


def products(value_ref, weight_ref, out_refs):
    t = lax.axis_index("tp")
    depth = weight_ref.shape[2]
    for pair in range(2):
        first, second = (t + 2 * pair) & 3, (t + 2 * pair + 1) & 3
        total = None
        for i in range(2):
            block = jnp.concatenate([weight_ref[first, i], weight_ref[second, i]], axis=1)
            term = mm(value_ref[:, i * depth : (i + 1) * depth], block)
            total = term if total is None else total + term
        out_refs[2 * pair][...] = total[:, :HEAD_DIM].astype(BF)
        out_refs[2 * pair + 1][...] = total[:, HEAD_DIM:].astype(BF)


def first_kernel(image_ref, *refs):
    pieces, out_refs, weight_ref = refs[:8], refs[8:12], refs[12]
    g, x = lax.axis_index("group"), lax.axis_index("fsdp_0")
    for r in range(4):
        source = (x + 4 - r) & 3
        for s in range(2):
            core = g if s == 0 else 1 - g
            weight_ref[2 * (source >> 1) + core, source & 1] = pieces[4 * s + r][...]
    products(image_ref, weight_ref, out_refs)


def terms_kernel(text_ref, weight_ref, *out_refs):
    products(text_ref, weight_ref, out_refs)


def grads_kernel(back_ref, image_back_ref, weight_ref, text_ref, image_ref):
    step = pl.program_id(0)

    def multiply(value_ref, out_ref):
        left = jnp.concatenate([value_ref[h] for h in range(4)], axis=1)
        depth = weight_ref.shape[2]
        for i in range(2):
            right = jnp.concatenate([weight_ref[h, i] for h in range(4)], axis=1)
            out_ref[:, i * depth : (i + 1) * depth] = lax.dot_general(
                left, right, (((1,), (1,)), ((), ())), preferred_element_type=F32
            ).astype(BF)

    @pl.when(step < 2)
    def _():
        multiply(back_ref, text_ref)

    @pl.when(step == 2)
    def _():
        multiply(image_back_ref, image_ref)


def give_kernel(
    text_ref, image_ref, back_hbm, p0, p1, p2, p3, give_ref, keep_ref, image_back_ref, back_ref, left_ref, sems
):
    rows = text_ref.shape[0]

    @pl.when(pl.program_id(0) == 0)
    def _():
        g, t = lax.axis_index("group"), lax.axis_index("tp")
        loads = [pltpu.make_async_copy(back_hbm, back_ref, sems.at[4])]
        for k, piece in enumerate((p0, p1, p2, p3)):
            loads.append(pltpu.make_async_copy(piece, image_back_ref.at[(t + 4 - k) & 3], sems.at[k]))
        for load in loads:
            load.start()
        for load in loads:
            load.wait()
        for q in range(4):
            head = 2 * (q & 1) + (1 - g if q < 2 else g)
            part = slice(q * HEAD_DIM, (q + 1) * HEAD_DIM)
            left_ref[part, :rows] = flip(back_ref[head])
            left_ref[part, rows:] = flip(image_back_ref[head])

    total = mm(left_ref[:, :rows], text_ref[...]) + mm(left_ref[:, rows:], image_ref[...])
    for o in range(2):
        for z in range(4):
            columns = slice(z * HEAD_DIM, (z + 1) * HEAD_DIM)
            give_ref[o, 0, z] = total[o * HEAD_DIM : (o + 1) * HEAD_DIM, columns].astype(BF)
            keep_ref[o, 0, z] = total[(2 + o) * HEAD_DIM : (3 + o) * HEAD_DIM, columns].astype(BF)


def attach_kernel(keep_ref, given_ref, *out_refs):
    x = lax.axis_index("fsdp_0")
    for r, out_ref in enumerate(out_refs):
        to_x = (x + r) & 3
        out_ref[...] = (keep_ref[to_x].astype(F32) + given_ref[to_x].astype(F32)).astype(BF)


def join_kernel(*refs):
    pieces, keys, out_ref = refs[:4], refs[4:8], refs[8]
    size = HEAD_DIM
    out_ref[:, :size] = summed(pieces).astype(BF)
    for k, piece in enumerate(keys):
        out_ref[:, size + 16 * k : size + 16 * (k + 1)] = piece[...]


def finish_kernel(in_ref, grad_ref, keys_ref):
    size = HEAD_DIM
    total = in_ref[0, :size].astype(F32)
    for z in range(1, NZ):
        total = total + in_ref[z, :size].astype(F32)
    grad_ref[...] = total.T
    for z in range(NZ):
        keys_ref[64 * z : 64 * (z + 1)] = in_ref[z, size:]


def summed(refs):
    total = refs[0][...].astype(F32)
    for ref in refs[1:]:
        total = total + ref[...].astype(F32)
    return total


def place_kernel(owner_ref, *refs):
    image, sent_refs = summed(refs[:4]), refs[4:]
    rows = 128 * len(sent_refs)
    owner, rank = ranks(owner_ref, 0)
    owner_x, owner_z, away = parted(owner)
    steps = (owner_x + 4 - lax.axis_index("fsdp_0")) & 3
    line = steps * 128 + owner_z * 16 + away * 8 + rank
    down = lax.broadcasted_iota(I32, (rows, line.shape[1]), 0)
    sent = mm(ones_where(down == line), image.astype(BF)).astype(BF)
    for k, sent_ref in enumerate(sent_refs):
        sent_ref[...] = sent[128 * k : 128 * (k + 1)]


def keys_kernel(
    seq_ref, slot_ref, t0, t1, t2, t3, own_ref, far_ref, bias_ref, whole_ref, signed_ref, out_ref
):
    rows = out_ref.shape[0]
    column = jnp.broadcast_to(slot_ref[...], (HEAD_DIM, rows)).T
    slot = column[:, :1]
    source_x, source_z, away = parted(slot >> 3)
    steps = (lax.axis_index("fsdp_0") + 4 - source_x) & 3
    line = source_z * 64 + steps * 16 + away * 8 + (slot & 7)
    lanes = lax.broadcasted_iota(I32, (rows, rows), 1)
    crossed = (lax.broadcasted_iota(I32, (rows, HEAD_DIM), 0) >> 3) & 1
    came = jnp.where(crossed == 1, far_ref[...].astype(F32), own_ref[...].astype(F32)).astype(BF)
    placed = mm(ones_where(lanes == line), came)
    value = jnp.where(column >= 0, placed, summed((t0, t1, t2, t3))) + bias_ref[...]
    swapped = pltpu.roll(value, HEAD_DIM // 2, 1)
    for s in range(rows // LENGTH):
        part = slice(s * LENGTH, (s + 1) * LENGTH)
        live = lax.broadcasted_iota(I32, (LENGTH, HEAD_DIM), 0) < seq_ref[s]
        turned = value[part] * whole_ref[...] + swapped[part] * signed_ref[...]
        out_ref[part] = jnp.where(live, turned, 0.0).astype(BF)


def per_device(
    text_embeds, image_embeds, key_weight, key_bias, key_cot, image_owner, image_slot, seq_lengths
):
    rows, columns = text_embeds.shape
    tokens = image_embeds.shape[0]
    slots = rows
    head = HEAD_DIM
    t = lax.axis_index("tp")
    whole, signed = tables()
    slot_row = image_slot.reshape(1, rows)
    owner_row = image_owner.reshape(1, tokens)

    fixed = lambda *dims: pl.BlockSpec(dims, lambda n: (0,) * len(dims))
    block = NZ * head

    own = lax.dynamic_slice_in_dim(key_weight, t * head, head, 1)
    piece = lax.ppermute(own, ALL, SPREAD)
    back, sent = kernel_call(
        back_kernel,
        out_shape=(shape(4, rows, head), shape(slots, head)),
        in_specs=[SMEM] + [VMEM] * 4,
        out_specs=(VMEM, VMEM),
        scratch_shapes=[pltpu.VMEM((4, rows, head), BF)],
        cost_estimate=cost(2 * rows * rows * head, 4 * rows * rows),
        name="back",
    )(seq_lengths, slot_row, key_cot, whole, signed)

    came = to_all(sent.reshape(slots // 8, 8, head), GROUP_FSDP).reshape(slots, head)
    taken = kernel_call(
        take_kernel,
        out_shape=shape(tokens, head),
        in_specs=[VMEM] * 2,
        out_specs=VMEM,
        cost_estimate=cost(2 * tokens * slots * head, 2 * slots * head),
        name="take",
    )(owner_row, came)

    load = jnp.broadcast_to(piece[None], (NZ, head, head))
    along_z = to_all(load, "fsdp_1")
    along_z = along_z.reshape(block, head)
    near = [along_z] + [shifted(along_z, "fsdp_0", k) for k in range(1, 4)]
    far = [lax.ppermute(one, "group", SWAP) for one in near]
    heads = [taken] + [shifted(taken, "tp", k) for k in range(1, 4)]

    chunk = columns // 4
    grid_block = pl.BlockSpec((2, 1, 4, head, head), lambda n: (0, n // 2, n % 2, 0, 0))
    give, keep, image_back = kernel_call(
        give_kernel,
        out_shape=(
            shape(2, 2, NZ, head, head),
            shape(2, 2, NZ, head, head),
            shape(4, tokens, head),
        ),
        grid=(4,),
        in_specs=[
            pl.BlockSpec((rows, chunk), lambda n: (0, n)),
            pl.BlockSpec((tokens, chunk), lambda n: (0, n)),
        ]
        + [pl.BlockSpec(memory_space=pltpu.HBM)] * 5,
        out_specs=(grid_block, grid_block, fixed(4, tokens, head)),
        scratch_shapes=[
            pltpu.VMEM((4, rows, head), BF),
            pltpu.VMEM((4 * head, rows + tokens), BF),
            pltpu.SemaphoreType.DMA((5,)),
        ],
        cost_estimate=cost(2 * (rows + tokens) * columns * 512, 4 * (rows + tokens) * columns),
        name="give",
    )(text_embeds, image_embeds, back, *heads)
    given = lax.ppermute(give, "group", SWAP)

    row_block = pl.BlockSpec((LENGTH, columns), lambda n: (jnp.minimum(n, 1), 0))
    image_block = pl.BlockSpec((tokens, columns), lambda n: (0, 0))
    weight_block = fixed(4, 2, block, head)
    product_cost = cost(2 * (rows + tokens) * columns * 512, 2 * (rows + tokens + 512) * columns)
    *image_parts, weight = kernel_call(
        first_kernel,
        out_shape=(shape(tokens, head),) * 4 + (shape(4, 2, block, head),),
        in_specs=[VMEM] * 9,
        out_specs=(VMEM,) * 5,
        cost_estimate=cost(2 * tokens * columns * 512, 2 * (tokens + 1024) * columns),
        name="first",
    )(image_embeds, *near, *far)
    image_parts = image_parts[:1] + [shifted(image_parts[k], "tp", k) for k in range(1, 4)]
    text_parts = kernel_call(
        terms_kernel,
        out_shape=(shape(rows, head),) * 4,
        grid=(2,),
        in_specs=[pl.BlockSpec((LENGTH, columns), lambda n: (n, 0)), weight_block],
        out_specs=(pl.BlockSpec((LENGTH, head), lambda n: (n, 0)),) * 4,
        cost_estimate=cost(2 * rows * columns * 512, 2 * (rows + 512) * columns),
        name="terms",
    )(text_embeds, weight)
    text_parts = [text_parts[0]] + [shifted(text_parts[k], "tp", k) for k in range(1, 4)]
    keys_sent = kernel_call(
        place_kernel,
        out_shape=(shape(head, head),) * 4,
        in_specs=[VMEM] * 5,
        out_specs=(VMEM,) * 4,
        cost_estimate=cost(2 * tokens * slots * head, 8 * tokens * head),
        name="place",
    )(owner_row, *image_parts)
    keys_sent = [keys_sent[0]] + [shifted(keys_sent[k], "fsdp_0", k) for k in range(1, 4)]

    kept = kernel_call(
        attach_kernel,
        out_shape=(shape(NZ, head, head),) * 4,
        in_specs=[VMEM] * 2,
        out_specs=(VMEM,) * 4,
        cost_estimate=cost(block * 4 * head, 32 * block * head),
        name="attach",
    )(keep.reshape(4, NZ, head, head), given.reshape(4, NZ, head, head))
    joined = kernel_call(
        join_kernel,
        out_shape=shape(NZ, head + 64, head),
        in_specs=[VMEM] * 8,
        out_specs=VMEM,
        cost_estimate=cost(block * 4 * head, 10 * block * head),
        name="join",
    )(
        kept[0],
        *[shifted(kept[k], "fsdp_0", k) for k in range(1, 4)],
        *[one.reshape(NZ, 16, head) for one in keys_sent],
    )
    over_z, keys_own = kernel_call(
        finish_kernel,
        out_shape=(shape(head, head, dtype=F32), shape(slots, head)),
        in_specs=[VMEM],
        out_specs=(VMEM, VMEM),
        cost_estimate=cost(block * head, 4 * block * head),
        name="finish",
    )(to_all(joined, "fsdp_1"))
    keys_far = lax.ppermute(keys_own, "group", SWAP)
    weight_grad = lax.ppermute(over_z, ALL, GATHER) / rows
    key_rows = kernel_call(
        keys_kernel,
        out_shape=shape(rows, head),
        in_specs=[SMEM] + [VMEM] * 10,
        out_specs=VMEM,
        cost_estimate=cost(2 * rows * slots * head, 8 * rows * head),
        name="keys",
    )(seq_lengths, slot_row, *text_parts, keys_own, keys_far, key_bias.reshape(1, head), whole, signed)

    text_grad, image_grad = kernel_call(
        grads_kernel,
        out_shape=(shape(rows, columns), shape(tokens, columns)),
        grid=(3,),
        in_specs=[
            pl.BlockSpec((4, LENGTH, head), lambda n: (0, jnp.minimum(n, 1), 0)),
            fixed(4, tokens, head),
            weight_block,
        ],
        out_specs=(row_block, image_block),
        cost_estimate=product_cost,
        name="grads",
    )(back, image_back, weight)

    return key_rows, text_grad, image_grad, weight_grad


def solution(mesh):
    split = Mesh(
        mesh.devices.reshape(mesh.shape["group"], NX, NZ, mesh.shape["tp"]),
        ("group", "fsdp_0", "fsdp_1", "tp"),
    )
    wide = P(GROUP_FSDP, "tp")
    return jax.shard_map(
        per_device,
        mesh=split,
        in_specs=(
            wide,
            wide,
            P(GROUP_FSDP, None),
            P("tp"),
            P(GROUP_FSDP, None),
            P(GROUP_FSDP),
            P(GROUP_FSDP),
            P(GROUP_FSDP),
        ),
        out_specs=(wide, wide, wide, wide),
        check_vma=False,
    )
```
